32 devices in a mesh: grp: 4 (over y, core), dev: 8 (over z, x).
Axes of the slice: x: 2, y: 2, z: 4, core: 2. Of those that a mesh axis runs over, the one named last changes fastest.
Arguments:
- embeddings: bfloat16 [8192, 768], P(('grp', 'dev')), may hold values from -6 to 6
- language: int32 [8192], P(('grp', 'dev')), may hold values from 0 to 108
- sentence_group: int32 [8192], P(('grp', 'dev')), may hold values from 0 to 2047
- pair_mask: int32 [109, 109], replicated, may hold values 0 or 1
Outputs:
- gradient: float32 [8192, 768], P(('grp', 'dev'))
The draws below stay inside these ranges and needn't reach their ends.
All inputs are finite; a program needn't handle non-finite values.
Results may differ from the reference program's by a relative error of at most 0.0012.
Values may be sent and summed in bfloat16 or wider, within the bound.
A program may use at most 256 MiB of HBM per device.

```python
import math
import jax
import jax.numpy as jnp
from jax import lax

D = 768
LANGS = 109
TOKENS = 8192
GROUPS = 2048


def set_ends(entries, key, least, high):
    spot = [jax.random.randint(jax.random.fold_in(key, axis), (), 0, length) for axis, length in enumerate(entries.shape)]
    main_axis = entries.shape.index(max(entries.shape))
    beside = spot[:main_axis] + [(spot[main_axis] + 1) % entries.shape[main_axis]] + spot[main_axis + 1:]
    return entries.at[tuple(spot)].set(least).at[tuple(beside)].set(high)


def level_of(rng, shape, split, least, top_value):
    gain, own = 1.0, jax.random.fold_in(rng, 6)
    for dim, parts in split:
        draws = jnp.exp(jax.random.uniform(jax.random.fold_in(own, dim), (parts,), jnp.float32, least / len(split), top_value / len(split)))
        gain = gain * jnp.repeat(draws, shape[dim] // parts).reshape([-1 if axis == dim else 1 for axis in range(len(shape))])
    return gain


def centred(stream_key, extent, deviation, reach, split=(), kind=jnp.bfloat16):
    array = jax.random.normal(stream_key, extent, jnp.float32) * deviation
    if len(split) > 0:
        array = level_of(stream_key, extent, split, -0.22, 0.18) * array
    return jnp.clip(array, min=-reach, max=reach).astype(kind)


def setup_inputs(seed: int = 0) -> dict:
    key_list = jax.random.split(jax.random.key(seed), 5)
    embeddings = centred(key_list[0], (TOKENS, D), 1.0, 6.0, ((0, 32),))
    language = set_ends(jax.random.randint(key_list[1], (TOKENS,), 0, LANGS), jax.random.fold_in(key_list[1], 1), 0, LANGS - 1).astype(jnp.int32)
    sentence_group = set_ends(jax.random.randint(key_list[2], (TOKENS,), 0, GROUPS), jax.random.fold_in(key_list[2], 1), 0, GROUPS - 1).astype(jnp.int32)
    pair_mask = set_ends((jax.random.randint(key_list[3], (LANGS, LANGS), 0, 4) < 3).astype(jnp.int32), jax.random.fold_in(key_list[3], 1), 0, 1)
    return {"embeddings": embeddings, "language": language, "sentence_group": sentence_group, "pair_mask": pair_mask}


def reference(embeddings, language, sentence_group, pair_mask):
    scale = 1.0 / math.sqrt(D)
    weight_table = (pair_mask + pair_mask.T).astype(jnp.float32) * 0.5
    lang_onehot = (language[:, None] == jnp.arange(LANGS, dtype=jnp.int32)[None, :]).astype(jnp.float32)
    weight_rows = jnp.dot(lang_onehot, weight_table, precision=lax.Precision.HIGHEST)
    block_rows = math.gcd(TOKENS, 512)
    column_index = jnp.arange(TOKENS, dtype=jnp.int32)

    def one_block(block_index):
        start = (block_index * block_rows).astype(jnp.int32)
        rows = lax.dynamic_slice_in_dim(embeddings, start, block_rows, 0)
        scores = jnp.dot(rows, embeddings.T, preferred_element_type=jnp.float32) * scale
        weight_values = jnp.dot(lax.dynamic_slice_in_dim(weight_rows, start, block_rows, 0), lang_onehot.T, precision=lax.Precision.HIGHEST)
        groups_here = lax.dynamic_slice_in_dim(sentence_group, start, block_rows, 0)
        labels = jnp.where(groups_here[:, None] == sentence_group[None, :], 1.0, -1.0).astype(jnp.float32)
        row_index = start + jnp.arange(block_rows, dtype=jnp.int32)
        offdiag = (row_index[:, None] != column_index[None, :]).astype(jnp.float32)
        coefficient = -weight_values * labels * jax.nn.sigmoid(-labels * scores) * scale * offdiag
        return jnp.dot(coefficient.astype(jnp.bfloat16), embeddings, preferred_element_type=jnp.float32)
    grads = lax.map(one_block, jnp.arange(TOKENS // block_rows, dtype=jnp.int32))
    return grads.reshape(TOKENS, D)
```

```python
import functools
import math

import jax
import jax.numpy as jnp
from jax import lax
from jax.experimental import pallas as pl
from jax.experimental.pallas import tpu as pltpu
from jax.sharding import PartitionSpec as P

MESH = pl.DeviceIdType.MESH


def kernel(groups, devs, e_hbm, m_hbm, mask_ref, out_ref, buf, mbuf, wr, gcol, send_sem, recv_sem, own_sem):
    rows, width = buf.shape[1], buf.shape[2]
    langs = mask_ref.shape[0]
    depth = devs // 2
    scale = 1.0 / math.sqrt(width)
    g, d = lax.axis_index("grp"), lax.axis_index("dev")
    core, y = g % 2, g // 2
    x, z = d % 2, d // 2
    me = g * devs + d
    half = rows // 2

    def block(yy, cc, zz, xx):
        return (yy * 2 + cc) * devs + zz * 2 + xx

    def view(ch, b):
        if ch == 0:
            return buf.at[b, pl.ds(0, half)]
        if ch == 1:
            return buf.at[b, pl.ds(half, half)]
        return mbuf.at[b]

    x_second = (True, False, True)
    channels = range(3)

    own_copies = [
        pltpu.make_async_copy(e_hbm, buf.at[me], own_sem.at[0]),
        pltpu.make_async_copy(m_hbm, mbuf.at[me], own_sem.at[1]),
    ]
    for c in own_copies:
        c.start()

    to_x, to_y, to_core = (g, d + 1 - 2 * x), (g + 2 - 4 * y, d), (g + 1 - 2 * core, d)
    up, down = (g, d + 2), (g, d - 2)
    has_up, has_down = z + 1 < depth, z > 0
    barrier = pltpu.get_barrier_semaphore()
    for target in (to_x, to_y, to_core):
        pl.semaphore_signal(barrier, inc=1, device_id=target, device_id_type=MESH)

    @pl.when(has_up)
    def _():
        pl.semaphore_signal(barrier, inc=1, device_id=up, device_id_type=MESH)

    @pl.when(has_down)
    def _():
        pl.semaphore_signal(barrier, inc=1, device_id=down, device_id_type=MESH)

    pl.semaphore_wait(barrier, 3 + has_up.astype(jnp.int32) + has_down.astype(jnp.int32))

    def copy(ch, way, b, target):
        return pltpu.make_async_remote_copy(
            src_ref=view(ch, b),
            dst_ref=view(ch, b),
            send_sem=send_sem.at[ch, way, b],
            recv_sem=recv_sem.at[ch, b],
            device_id=target,
            device_id_type=MESH,
        )

    def arrived(ch, b):
        copy(ch, 0, b, to_core).wait_recv()

    def act(ch, way, b, target, start):
        c = copy(ch, way, b, target)
        if start:
            c.start()
        else:
            c.wait_send()

    short = jnp.minimum(z, depth - 1 - z)
    long_sign = jnp.where(z * 2 < depth, 1, -1)

    def line(k):
        near = (k + 1) // 2
        sign = jnp.where(k % 2 == 1, long_sign, -long_sign)
        return jnp.where(k <= 2 * short, z + sign * near, z + long_sign * (k - short))

    def first(k, start):
        zz = line(k)
        b = block(y, core, zz, x)
        for ch in channels:
            if start:

                @pl.when(k > 0)
                def _():
                    arrived(ch, b)

            @pl.when(jnp.logical_and(zz <= z, has_up))
            def _():
                act(ch, 0, b, up, start)

            @pl.when(jnp.logical_and(zz >= z, has_down))
            def _():
                act(ch, 1, b, down, start)

            act(ch, 2, b, to_x if x_second[ch] else to_y, start)
            act(ch, 3, b, to_y if x_second[ch] else to_x, start)
            act(ch, 4, b, to_core, start)

    def second(k, start):
        zz = line(k)
        for ch in channels:
            b = block(y, core, zz, 1 - x) if x_second[ch] else block(1 - y, core, zz, x)
            if start:
                arrived(ch, b)
            act(ch, 3, b, to_y if x_second[ch] else to_x, start)
            act(ch, 4, b, to_core, start)

    def third(k, start):
        zz = line(k)
        for last in range(2):
            for ch in channels:
                if last:
                    b = block(1 - y, core, zz, 1 - x)
                else:
                    b = block(1 - y, core, zz, x) if x_second[ch] else block(y, core, zz, 1 - x)
                if start:
                    arrived(ch, b)
                act(ch, 4, b, to_core, start)

    for c in own_copies:
        c.wait()
    first(0, True)

    lang_axis = lax.broadcasted_iota(jnp.int32, (langs, rows), 0)
    table = mask_ref[...].astype(jnp.float32)
    table = ((table + table.T) * 0.5).astype(jnp.bfloat16)
    own_hot = (lang_axis == mbuf[me, 0:1, :]).astype(jnp.float32).astype(jnp.bfloat16)
    wr[...] = lax.dot_general(
        own_hot, table, (((0,), (0,)), ((), ())), preferred_element_type=jnp.float32
    ).astype(jnp.bfloat16)
    gcol[...] = jnp.broadcast_to(mbuf[me, 1:2, :].astype(jnp.float32), (128, rows)).T
    out_ref[...] = jnp.zeros_like(out_ref)

    def compute(b):
        cols = buf[b]
        scores = lax.dot_general(
            buf[me], cols, (((1,), (1,)), ((), ())), preferred_element_type=jnp.float32
        )
        hot = (lang_axis == mbuf[b, 0:1, :]).astype(jnp.float32).astype(jnp.bfloat16)
        weight = jnp.dot(wr[...], hot, preferred_element_type=jnp.float32)
        own_group = jnp.concatenate([gcol[...]] * (rows // 128), axis=1)
        same = own_group == mbuf[b, 1:2, :].astype(jnp.float32)
        power = jnp.minimum(jnp.where(same, scores, -scores) * (scale * math.log2(math.e)), 127.9)
        signed = jnp.where(same, -weight, weight)
        coef = signed * (scale / (1.0 + jnp.exp2(power)))
        apart = lax.broadcasted_iota(jnp.int32, (rows, rows), 0) - lax.broadcasted_iota(
            jnp.int32, (rows, rows), 1
        )
        coef = jnp.where(apart == (b - me) * rows, 0.0, coef).astype(jnp.bfloat16)
        out_ref[...] += jnp.dot(coef, cols, preferred_element_type=jnp.float32)

    def step(k, carry):
        @pl.when(k < depth)
        def _():
            first(k, True)

        @pl.when(k <= depth)
        def _():
            second(k - 1, True)

        @pl.when(k >= 2)
        def _():
            third(k - 2, True)
            zz = line(k - 2)

            def one(j, carry):
                yy = (y + j // 2) % 2
                xx = (x + j) % 2
                cc = (core + j // 4) % 2
                b = block(yy, cc, zz, xx)

                @pl.when(j >= 4)
                def _():
                    for ch in channels:
                        arrived(ch, b)

                compute(b)
                return carry

            lax.fori_loop(0, 8, one, 0)

        return carry

    lax.fori_loop(1, depth + 2, step, 0)

    def drain(k, carry):
        first(k, False)
        second(k, False)
        third(k, False)
        return carry

    lax.fori_loop(0, depth, drain, 0)


def on_device(groups, devs, embeddings, language, sentence_group, pair_mask):
    rows, width = embeddings.shape
    count = groups * devs
    langs = pair_mask.shape[0]
    meta = jnp.stack([language, sentence_group])
    return pl.pallas_call(
        functools.partial(kernel, groups, devs),
        out_shape=jax.ShapeDtypeStruct((rows, width), jnp.float32),
        in_specs=[
            pl.BlockSpec(memory_space=pl.ANY),
            pl.BlockSpec(memory_space=pl.ANY),
            pl.BlockSpec(memory_space=pltpu.VMEM),
        ],
        out_specs=pl.BlockSpec(memory_space=pltpu.VMEM),
        scratch_shapes=[
            pltpu.VMEM((count, rows, width), jnp.bfloat16),
            pltpu.VMEM((count, 2, rows), jnp.int32),
            pltpu.VMEM((rows, langs), jnp.bfloat16),
            pltpu.VMEM((rows, 128), jnp.float32),
            pltpu.SemaphoreType.DMA((3, 5, count)),
            pltpu.SemaphoreType.DMA((3, count)),
            pltpu.SemaphoreType.DMA((2,)),
        ],
        compiler_params=pltpu.CompilerParams(
            collective_id=0, has_side_effects=True, vmem_limit_bytes=64 * 1000 * 1000
        ),
    )(embeddings, meta, pair_mask)


def solution(mesh):
    groups, devs = mesh.shape["grp"], mesh.shape["dev"]
    return jax.shard_map(
        functools.partial(on_device, groups, devs),
        mesh=mesh,
        in_specs=(P(("grp", "dev"), None), P(("grp", "dev")), P(("grp", "dev")), P()),
        out_specs=P(("grp", "dev"), None),
        check_vma=False,
    )
```

```python
import functools
import math

import jax
import jax.numpy as jnp
from jax import lax
from jax.experimental import pallas as pl
from jax.experimental.pallas import tpu as pltpu
from jax.sharding import PartitionSpec as P

MESH = pl.DeviceIdType.MESH


def kernel(groups, devs, e_hbm, m_hbm, mask_ref, out_ref, buf, mbuf, wr, gcol, send_sem, recv_sem, own_sem):
    rows, width = buf.shape[1], buf.shape[2]
    langs = mask_ref.shape[0]
    depth = devs // 2
    scale = 1.0 / math.sqrt(width)
    g, d = lax.axis_index("grp"), lax.axis_index("dev")
    core, y = g % 2, g // 2
    x, z = d % 2, d // 2
    me = g * devs + d
    half = rows // 2

    def block(yy, cc, zz, xx):
        return (yy * 2 + cc) * devs + zz * 2 + xx

    def view(ch, b):
        if ch == 0:
            return buf.at[b, pl.ds(0, half)]
        if ch == 1:
            return buf.at[b, pl.ds(half, half)]
        return mbuf.at[b]

    x_second = (True, False, True)
    channels = range(3)

    own_copies = [
        pltpu.make_async_copy(e_hbm, buf.at[me], own_sem.at[0]),
        pltpu.make_async_copy(m_hbm, mbuf.at[me], own_sem.at[1]),
    ]
    for c in own_copies:
        c.start()

    to_x, to_y, to_core = (g, d + 1 - 2 * x), (g + 2 - 4 * y, d), (g + 1 - 2 * core, d)
    up, down = (g, d + 2), (g, d - 2)
    has_up, has_down = z + 1 < depth, z > 0
    barrier = pltpu.get_barrier_semaphore()
    for target in (to_x, to_y, to_core):
        pl.semaphore_signal(barrier, inc=1, device_id=target, device_id_type=MESH)

    @pl.when(has_up)
    def _():
        pl.semaphore_signal(barrier, inc=1, device_id=up, device_id_type=MESH)

    @pl.when(has_down)
    def _():
        pl.semaphore_signal(barrier, inc=1, device_id=down, device_id_type=MESH)

    pl.semaphore_wait(barrier, 3 + has_up.astype(jnp.int32) + has_down.astype(jnp.int32))

    def copy(ch, way, b, target):
        return pltpu.make_async_remote_copy(
            src_ref=view(ch, b),
            dst_ref=view(ch, b),
            send_sem=send_sem.at[ch, way, b],
            recv_sem=recv_sem.at[ch, b],
            device_id=target,
            device_id_type=MESH,
        )

    def arrived(ch, b):
        copy(ch, 0, b, to_core).wait_recv()

    def act(ch, way, b, target, start):
        c = copy(ch, way, b, target)
        if start:
            c.start()
        else:
            c.wait_send()

    short = jnp.minimum(z, depth - 1 - z)
    long_sign = jnp.where(z * 2 < depth, 1, -1)

    def line(k):
        near = (k + 1) // 2
        sign = jnp.where(k % 2 == 1, long_sign, -long_sign)
        return jnp.where(k <= 2 * short, z + sign * near, z + long_sign * (k - short))

    def first(k, start):
        zz = line(k)
        b = block(y, core, zz, x)
        for ch in channels:
            if start:

                @pl.when(k > 0)
                def _():
                    arrived(ch, b)

            @pl.when(jnp.logical_and(zz <= z, has_up))
            def _():
                act(ch, 0, b, up, start)

            @pl.when(jnp.logical_and(zz >= z, has_down))
            def _():
                act(ch, 1, b, down, start)

            act(ch, 2, b, to_x if x_second[ch] else to_y, start)
            act(ch, 3, b, to_y if x_second[ch] else to_x, start)
            act(ch, 4, b, to_core, start)

    def second(k, start):
        zz = line(k)
        for ch in channels:
            b = block(y, core, zz, 1 - x) if x_second[ch] else block(1 - y, core, zz, x)
            if start:
                arrived(ch, b)
            act(ch, 3, b, to_y if x_second[ch] else to_x, start)
            act(ch, 4, b, to_core, start)

    def third(k, last, start):
        zz = line(k)
        for ch in channels:
            if last:
                b = block(1 - y, core, zz, 1 - x)
            else:
                b = block(1 - y, core, zz, x) if x_second[ch] else block(y, core, zz, 1 - x)
            if start:
                arrived(ch, b)
            act(ch, 4, b, to_core, start)

    for c in own_copies:
        c.wait()
    first(0, True)

    lang_axis = lax.broadcasted_iota(jnp.int32, (langs, rows), 0)
    table = mask_ref[...].astype(jnp.float32)
    table = ((table + table.T) * 0.5).astype(jnp.bfloat16)
    own_hot = (lang_axis == mbuf[me, 0:1, :]).astype(jnp.float32).astype(jnp.bfloat16)
    wr[...] = lax.dot_general(
        own_hot, table, (((0,), (0,)), ((), ())), preferred_element_type=jnp.float32
    ).astype(jnp.bfloat16)
    gcol[...] = jnp.broadcast_to(mbuf[me, 1:2, :].astype(jnp.float32), (128, rows)).T
    out_ref[...] = jnp.zeros_like(out_ref)

    own_group = jnp.concatenate([gcol[...]] * (rows // 128), axis=1)

    def coefficients(b, diagonal):
        scores = lax.dot_general(
            buf[me], buf[b], (((1,), (1,)), ((), ())), preferred_element_type=jnp.float32
        )
        hot = (lang_axis == mbuf[b, 0:1, :]).astype(jnp.float32).astype(jnp.bfloat16)
        weight = jnp.dot(wr[...], hot, preferred_element_type=jnp.float32)
        same = own_group == mbuf[b, 1:2, :].astype(jnp.float32)
        power = jnp.minimum(jnp.where(same, scores, -scores) * (scale * math.log2(math.e)), 127.9)
        signed = jnp.where(same, -weight, weight)
        coef = signed * (scale / (1.0 + jnp.exp2(power)))
        if diagonal:
            apart = lax.broadcasted_iota(jnp.int32, (rows, rows), 0) - lax.broadcasted_iota(
                jnp.int32, (rows, rows), 1
            )
            coef = jnp.where(apart == (b - me) * rows, 0.0, coef)
        return coef.astype(jnp.bfloat16)

    def compute(blocks, diagonal=False):
        total = None
        for b in blocks:
            part = jnp.dot(
                coefficients(b, diagonal), buf[b], preferred_element_type=jnp.float32
            )
            total = part if total is None else total + part
        out_ref[...] += total

    def near_pair(k):
        zz = line(k)
        own, other = block(y, core, zz, x), block(y, 1 - core, zz, x)
        for ch in channels:
            arrived(ch, other)
        compute((own, other), True)

    def side_pair(k, cc, wait):
        zz = line(k)
        pair = (block(y, cc, zz, 1 - x), block(1 - y, cc, zz, x))

        if wait is not None:

            @pl.when(wait)
            def _():
                for b in pair:
                    for ch in channels:
                        arrived(ch, b)

        compute(pair)

    def far_block(k, cc, wait):
        b = block(1 - y, cc, line(k), 1 - x)

        @pl.when(wait)
        def _():
            for ch in channels:
                arrived(ch, b)

        compute((b,))

    def step(k, carry):
        @pl.when(k < depth)
        def _():
            first(k, True)

        @pl.when(k <= depth)
        def _():
            second(k - 1, True)
            near_pair(k - 1)

        @pl.when(k >= 2)
        def _():
            third(k - 2, 0, True)

            def side(j, carry):
                side_pair(k - 2, (core + j) % 2, j > 0)
                return carry

            lax.fori_loop(0, 2, side, 0)
            third(k - 2, 1, True)

            def far(j, carry):
                far_block(k - 2, (core + j) % 2, j > 0)
                return carry

            lax.fori_loop(0, 2, far, 0)

        return carry

    lax.fori_loop(1, depth + 2, step, 0)

    def drain(k, carry):
        first(k, False)
        second(k, False)
        third(k, 0, False)
        third(k, 1, False)
        return carry

    lax.fori_loop(0, depth, drain, 0)


def on_device(groups, devs, embeddings, language, sentence_group, pair_mask):
    rows, width = embeddings.shape
    count = groups * devs
    langs = pair_mask.shape[0]
    meta = jnp.stack([language, sentence_group])
    return pl.pallas_call(
        functools.partial(kernel, groups, devs),
        out_shape=jax.ShapeDtypeStruct((rows, width), jnp.float32),
        in_specs=[
            pl.BlockSpec(memory_space=pl.ANY),
            pl.BlockSpec(memory_space=pl.ANY),
            pl.BlockSpec(memory_space=pltpu.VMEM),
        ],
        out_specs=pl.BlockSpec(memory_space=pltpu.VMEM),
        scratch_shapes=[
            pltpu.VMEM((count, rows, width), jnp.bfloat16),
            pltpu.VMEM((count, 2, rows), jnp.int32),
            pltpu.VMEM((rows, langs), jnp.bfloat16),
            pltpu.VMEM((rows, 128), jnp.float32),
            pltpu.SemaphoreType.DMA((3, 5, count)),
            pltpu.SemaphoreType.DMA((3, count)),
            pltpu.SemaphoreType.DMA((2,)),
        ],
        compiler_params=pltpu.CompilerParams(
            collective_id=0, has_side_effects=True, vmem_limit_bytes=64 * 1000 * 1000
        ),
    )(embeddings, meta, pair_mask)


def solution(mesh):
    groups, devs = mesh.shape["grp"], mesh.shape["dev"]
    return jax.shard_map(
        functools.partial(on_device, groups, devs),
        mesh=mesh,
        in_specs=(P(("grp", "dev"), None), P(("grp", "dev")), P(("grp", "dev")), P()),
        out_specs=P(("grp", "dev"), None),
        check_vma=False,
    )
```

```python
import functools
import math

import jax
import jax.numpy as jnp
from jax import lax
from jax.experimental import pallas as pl
from jax.experimental.pallas import tpu as pltpu
from jax.sharding import PartitionSpec as P

MESH = pl.DeviceIdType.MESH


def kernel(groups, devs, e_hbm, l_hbm, g_hbm, mask_ref, out_ref, buf, mbuf, wr, gcol, send_sem, recv_sem, own_sem):
    rows, width = buf.shape[1], buf.shape[2]
    langs = mask_ref.shape[0]
    depth = devs // 2
    scale = 1.0 / math.sqrt(width)
    g, d = lax.axis_index("grp"), lax.axis_index("dev")
    core, y = g % 2, g // 2
    x, z = d % 2, d // 2
    me = g * devs + d
    half = rows // 2

    def block(yy, cc, zz, xx):
        return (yy * 2 + cc) * devs + zz * 2 + xx

    def view(ch, b):
        if ch == 0:
            return buf.at[b, pl.ds(0, half)]
        if ch == 1:
            return buf.at[b, pl.ds(half, half)]
        return mbuf.at[b]

    x_second = (True, False, True)
    channels = range(3)

    own_copies = [
        pltpu.make_async_copy(e_hbm, buf.at[me], own_sem.at[0]),
        pltpu.make_async_copy(l_hbm, mbuf.at[me, pl.ds(0, 1)], own_sem.at[1]),
        pltpu.make_async_copy(g_hbm, mbuf.at[me, pl.ds(1, 1)], own_sem.at[2]),
    ]
    for c in own_copies:
        c.start()

    to_x, to_y, to_core = (g, d + 1 - 2 * x), (g + 2 - 4 * y, d), (g + 1 - 2 * core, d)
    up, down = (g, d + 2), (g, d - 2)
    has_up, has_down = z + 1 < depth, z > 0
    barrier = pltpu.get_barrier_semaphore()
    for target in (to_x, to_y, to_core):
        pl.semaphore_signal(barrier, inc=1, device_id=target, device_id_type=MESH)

    @pl.when(has_up)
    def _():
        pl.semaphore_signal(barrier, inc=1, device_id=up, device_id_type=MESH)

    @pl.when(has_down)
    def _():
        pl.semaphore_signal(barrier, inc=1, device_id=down, device_id_type=MESH)

    pl.semaphore_wait(barrier, 3 + has_up.astype(jnp.int32) + has_down.astype(jnp.int32))

    def copy(ch, way, b, target):
        return pltpu.make_async_remote_copy(
            src_ref=view(ch, b),
            dst_ref=view(ch, b),
            send_sem=send_sem.at[ch, way, b],
            recv_sem=recv_sem.at[ch, b],
            device_id=target,
            device_id_type=MESH,
        )

    def arrived(ch, b):
        copy(ch, 0, b, to_core).wait_recv()

    def act(ch, way, b, target, start):
        c = copy(ch, way, b, target)
        if start:
            c.start()
        else:
            c.wait_send()

    short = jnp.minimum(z, depth - 1 - z)
    long_sign = jnp.where(z * 2 < depth, 1, -1)

    def line(k):
        near = (k + 1) // 2
        sign = jnp.where(k % 2 == 1, long_sign, -long_sign)
        return jnp.where(k <= 2 * short, z + sign * near, z + long_sign * (k - short))

    def first(k, start):
        zz = line(k)
        b = block(y, core, zz, x)
        for ch in channels:
            if start:

                @pl.when(k > 0)
                def _():
                    arrived(ch, b)

            @pl.when(jnp.logical_and(zz <= z, has_up))
            def _():
                act(ch, 0, b, up, start)

            @pl.when(jnp.logical_and(zz >= z, has_down))
            def _():
                act(ch, 1, b, down, start)

            act(ch, 2, b, to_x if x_second[ch] else to_y, start)
            act(ch, 3, b, to_y if x_second[ch] else to_x, start)
            act(ch, 4, b, to_core, start)

    def second(k, start):
        zz = line(k)
        for ch in channels:
            b = block(y, core, zz, 1 - x) if x_second[ch] else block(1 - y, core, zz, x)
            if start:
                arrived(ch, b)
            act(ch, 3, b, to_y if x_second[ch] else to_x, start)
            act(ch, 4, b, to_core, start)

    def third(k, last, start):
        zz = line(k)
        for ch in channels:
            if last:
                b = block(1 - y, core, zz, 1 - x)
            else:
                b = block(1 - y, core, zz, x) if x_second[ch] else block(y, core, zz, 1 - x)
            if start:
                arrived(ch, b)
            act(ch, 4, b, to_core, start)

    for c in own_copies:
        c.wait()
    first(0, True)

    lang_axis = lax.broadcasted_iota(jnp.int32, (langs, rows), 0)
    table = mask_ref[...].astype(jnp.float32)
    table = ((table + table.T) * 0.5).astype(jnp.bfloat16)
    own_hot = (lang_axis == mbuf[me, 0:1, :]).astype(jnp.float32).astype(jnp.bfloat16)
    wr[...] = lax.dot_general(
        own_hot, table, (((0,), (0,)), ((), ())), preferred_element_type=jnp.float32
    ).astype(jnp.bfloat16)
    gcol[...] = jnp.broadcast_to(mbuf[me, 1:2, :].astype(jnp.float32), (128, rows)).T
    out_ref[...] = jnp.zeros_like(out_ref)

    own_group = jnp.concatenate([gcol[...]] * (rows // 128), axis=1)

    def coefficients(b, diagonal):
        scores = lax.dot_general(
            buf[me], buf[b], (((1,), (1,)), ((), ())), preferred_element_type=jnp.float32
        )
        hot = (lang_axis == mbuf[b, 0:1, :]).astype(jnp.float32).astype(jnp.bfloat16)
        weight = jnp.dot(wr[...], hot, preferred_element_type=jnp.float32)
        same = own_group == mbuf[b, 1:2, :].astype(jnp.float32)
        power = jnp.minimum(jnp.where(same, scores, -scores) * (scale * math.log2(math.e)), 127.9)
        signed = jnp.where(same, -weight, weight)
        coef = signed * (scale / (1.0 + jnp.exp2(power)))
        if diagonal:
            apart = lax.broadcasted_iota(jnp.int32, (rows, rows), 0) - lax.broadcasted_iota(
                jnp.int32, (rows, rows), 1
            )
            coef = jnp.where(apart == (b - me) * rows, 0.0, coef)
        return coef.astype(jnp.bfloat16)

    def compute(blocks, diagonal=False):
        total = None
        for b in blocks:
            part = jnp.dot(
                coefficients(b, diagonal), buf[b], preferred_element_type=jnp.float32
            )
            total = part if total is None else total + part
        out_ref[...] += total

    def near_pair(k):
        zz = line(k)
        own, other = block(y, core, zz, x), block(y, 1 - core, zz, x)
        for ch in channels:
            arrived(ch, other)
        compute((own, other), True)

    def side_pair(k, cc, wait):
        zz = line(k)
        pair = (block(y, cc, zz, 1 - x), block(1 - y, cc, zz, x))

        if wait is not None:

            @pl.when(wait)
            def _():
                for b in pair:
                    for ch in channels:
                        arrived(ch, b)

        compute(pair)

    def far_block(k, cc, wait):
        b = block(1 - y, cc, line(k), 1 - x)

        @pl.when(wait)
        def _():
            for ch in channels:
                arrived(ch, b)

        compute((b,))

    def step(k, carry):
        @pl.when(k < depth)
        def _():
            first(k, True)

        @pl.when(k <= depth)
        def _():
            second(k - 1, True)
            near_pair(k - 1)

        @pl.when(k >= 2)
        def _():
            third(k - 2, 0, True)

            def side(j, carry):
                side_pair(k - 2, (core + j) % 2, j > 0)
                return carry

            lax.fori_loop(0, 2, side, 0)
            third(k - 2, 1, True)

            def far(j, carry):
                far_block(k - 2, (core + j) % 2, j > 0)
                return carry

            lax.fori_loop(0, 2, far, 0)

        return carry

    lax.fori_loop(1, depth + 2, step, 0)

    def drain(k, carry):
        first(k, False)
        second(k, False)
        third(k, 0, False)
        third(k, 1, False)
        return carry

    lax.fori_loop(0, depth, drain, 0)


def on_device(groups, devs, embeddings, language, sentence_group, pair_mask):
    rows, width = embeddings.shape
    count = groups * devs
    langs = pair_mask.shape[0]
    return pl.pallas_call(
        functools.partial(kernel, groups, devs),
        out_shape=jax.ShapeDtypeStruct((rows, width), jnp.float32),
        in_specs=[
            pl.BlockSpec(memory_space=pl.ANY),
            pl.BlockSpec(memory_space=pl.ANY),
            pl.BlockSpec(memory_space=pl.ANY),
            pl.BlockSpec(memory_space=pltpu.VMEM),
        ],
        out_specs=pl.BlockSpec(memory_space=pltpu.VMEM),
        scratch_shapes=[
            pltpu.VMEM((count, rows, width), jnp.bfloat16),
            pltpu.VMEM((count, 2, rows), jnp.int32),
            pltpu.VMEM((rows, langs), jnp.bfloat16),
            pltpu.VMEM((rows, 128), jnp.float32),
            pltpu.SemaphoreType.DMA((3, 5, count)),
            pltpu.SemaphoreType.DMA((3, count)),
            pltpu.SemaphoreType.DMA((3,)),
        ],
        compiler_params=pltpu.CompilerParams(
            collective_id=0, has_side_effects=True, vmem_limit_bytes=64 * 1000 * 1000
        ),
    )(embeddings, language.reshape(1, rows), sentence_group.reshape(1, rows), pair_mask)


def solution(mesh):
    groups, devs = mesh.shape["grp"], mesh.shape["dev"]
    return jax.shard_map(
        functools.partial(on_device, groups, devs),
        mesh=mesh,
        in_specs=(P(("grp", "dev"), None), P(("grp", "dev")), P(("grp", "dev")), P()),
        out_specs=P(("grp", "dev"), None),
        check_vma=False,
    )
```
